32 devices in a mesh: st: 8 (over y, x, core), fq: 4 (over z).
Axes of the slice: x: 2, y: 2, z: 4, core: 2. Of those that a mesh axis runs over, the one named last changes fastest.
Arguments:
- signals: bfloat16 [512, 16384], P(('st', 'fq')), may hold values from -6 to 6
- freq_bins: int32 [1024], replicated, may hold values from 1 to 8191, as said below
- sensor_station: int32 [512], P('st'), may hold values from 0 to 255, as said below
- gain: bfloat16 [512, 768], P('st'), may hold values from -1.5 to 1.5
- damping: float32 [256, 768], P('st'), may hold values from 0 to 1
- damping_up: float32 [256, 768], P('st'), may hold values from 0 to 1
- phase_speed: float32 [768], replicated, may hold values from 0.5 to 4
Outputs:
- estimate: bfloat16 [256, 768, 1024], P(('st', 'fq'))
The draws below stay inside these ranges and needn't reach their ends.
Inputs may be any that keep to these rules, and one draw needn't show every extreme that they name: `freq_bins`: distinct bin numbers. `sensor_station`: sensor s sits at one of the 32 stations starting at (s // 64) * 32.
All inputs are finite; a program needn't handle non-finite values.
Results may differ from the reference program's by a relative error of at most 0.015.
Values may be sent and summed in bfloat16 or wider, within the bound.
A program may use at most 320 MiB of HBM per device.

```python
import math
import jax
import jax.numpy as jnp
from jax import lax

NT = 16384
M = 768
NF = 1024
ST_DEV = 32
SENS_GRP = 64
TOUT = 1024
STATIONS = 256
SENS = 512


def draw_freq_bins(key, part):
    order = jax.random.permutation(jax.random.fold_in(key, 11), NT // 2 - 1)
    return (order[:NF] + 1).astype(jnp.int32)


def draw_sensor_station(key, part):
    groups = jnp.arange(SENS, dtype=jnp.int32) // SENS_GRP
    offsets = jax.random.randint(jax.random.fold_in(key, 23), (SENS,), 0, ST_DEV, dtype=jnp.int32)
    return (groups * ST_DEV + offsets).astype(jnp.int32)


def decay_table(key):
    keys = jax.random.split(key, 7)
    share = 0.5
    fast = jax.random.uniform(keys[0], (M,)) < share
    fast_rate = jax.random.uniform(keys[1], (M,), minval=2.3 / (0.75 * ST_DEV), maxval=2.3 / (0.5 * ST_DEV))
    slow_rate = jax.random.uniform(keys[2], (M,), minval=0.1, maxval=0.5) * (2.3 / STATIONS)
    rate = jnp.where(fast, fast_rate, slow_rate)
    blocks = jnp.arange(STATIONS, dtype=jnp.int32) // ST_DEV
    block_factor = jnp.exp(jax.random.uniform(keys[3], (STATIONS // ST_DEV,), minval=-0.35, maxval=0.35))
    station_factor = jax.random.uniform(keys[4], (STATIONS, 1), minval=0.8, maxval=1.2)
    damping_coefficients = rate[None, :] * block_factor[blocks][:, None] * station_factor
    probe_positions = jax.random.randint(keys[5], (2,), 0, STATIONS, dtype=jnp.int32)
    boundary_distances = jax.random.uniform(keys[6], (2,), minval=0.55, maxval=0.8)
    measurement_planes = jnp.arange(STATIONS, dtype=jnp.int32)
    excitation_pulse = jnp.where(measurement_planes == probe_positions[0], boundary_distances[0], 1.0) * jnp.where(measurement_planes == probe_positions[1], boundary_distances[1], 1.0)
    return (jnp.exp(-damping_coefficients) * excitation_pulse[:, None]).astype(jnp.float32)


def draw_damping(key, part):
    return decay_table(jax.random.fold_in(key, 101))


def draw_damping_up(key, part):
    return decay_table(jax.random.fold_in(key, 202))


def shard_levels(rng, extent, pieces, smallest, top_value):
    level = 1.0
    for position, parts in pieces:
        heights = jax.random.uniform(jax.random.fold_in(jax.random.fold_in(rng, 6), position), (parts,), jnp.float32, smallest / len(pieces), top_value / len(pieces))
        level = level * jnp.repeat(jnp.exp(heights), extent[position] // parts).reshape((-1,) + (1,) * (len(extent) - 1 - position))
    return level


def centred(stream_key, extent, spread, most, cuts=(), kind=jnp.bfloat16):
    loudness = shard_levels(stream_key, extent, cuts, -0.22, 0.18) if cuts else 1.0
    entries = jax.random.normal(stream_key, extent, jnp.float32) * spread * loudness
    return jnp.minimum(jnp.maximum(entries, -most), most).astype(kind)


def setup_inputs(seed: int = 0) -> dict:
    key_of = jax.random.split(jax.random.key(seed), 8)
    signals = centred(key_of[0], (SENS, NT), 1.0, 6.0, ((0, 32),))
    freq_bins = draw_freq_bins(jax.random.fold_in(key_of[7], 71), 0)
    sensor_station = draw_sensor_station(jax.random.fold_in(key_of[7], 71), 0)
    gain = centred(key_of[3], (SENS, M), 16 ** -0.5, 1.5, ((0, 8),))
    damping = draw_damping(jax.random.fold_in(key_of[7], 71), 0)
    damping_up = draw_damping_up(jax.random.fold_in(key_of[7], 71), 0)
    phase_speed = jnp.clip(jnp.exp(jax.random.uniform(key_of[6], (M,), jnp.float32, math.log(0.5), math.log(4.0))), 0.5, 4.0)
    return {"signals": signals, "freq_bins": freq_bins, "sensor_station": sensor_station, "gain": gain, "damping": damping, "damping_up": damping_up, "phase_speed": phase_speed}


def cmul(left, right):
    return jnp.stack([left[0] * right[0] - left[1] * right[1], left[0] * right[1] + left[1] * right[0]])

def reference(signals, freq_bins, sensor_station, gain, damping, damping_up, phase_speed):
    n_blocks = STATIONS // ST_DEV
    times = lax.iota(jnp.int32, NT)
    hann = 0.5 - 0.5 * jnp.cos(times.astype(jnp.float32) * (2 * math.pi / NT))
    windowed = (signals.astype(jnp.float32) * hann[None, :]).astype(jnp.bfloat16)
    angle = (times[:, None] * freq_bins[None, :] % NT).astype(jnp.float32) * (2 * math.pi / NT)
    cos_table = (jnp.cos(angle) / math.sqrt(NT)).astype(jnp.bfloat16)
    sin_table = (jnp.sin(angle) / math.sqrt(NT)).astype(jnp.bfloat16)
    spec_re = jnp.dot(windowed, cos_table, preferred_element_type=jnp.float32).astype(jnp.bfloat16)
    spec_im = (-jnp.dot(windowed, sin_table, preferred_element_type=jnp.float32)).astype(jnp.bfloat16)
    theta = 2 * math.pi * (freq_bins.astype(jnp.float32) / NT)[:, None] * phase_speed[None, :]
    rot_down = jnp.stack([jnp.cos(theta), -jnp.sin(theta)])
    rot_up = jnp.stack([jnp.cos(theta), jnp.sin(theta)])
    spectra = jnp.stack([spec_re, spec_im]).astype(jnp.float32)
    gain_wide = gain.astype(jnp.float32)
    zeros = jnp.zeros((2, NF, M), jnp.float32)
    t_out = NT - TOUT + lax.iota(jnp.int32, TOUT)
    out_angle = (freq_bins[:, None] * t_out[None, :] % NT).astype(jnp.float32) * (2 * math.pi / NT)
    inverse = jnp.stack([jnp.cos(out_angle) / math.sqrt(NF), -jnp.sin(out_angle) / math.sqrt(NF)]).astype(jnp.bfloat16)

    def block_forcing(block):
        first = (block * SENS_GRP).astype(jnp.int32)
        spec_block = lax.dynamic_slice_in_dim(spectra, first, SENS_GRP, 1)
        gain_block = lax.dynamic_slice_in_dim(gain_wide, first, SENS_GRP, 0)
        local = lax.dynamic_slice_in_dim(sensor_station, first, SENS_GRP, 0) - block * ST_DEV
        outer = jnp.transpose(spec_block, (1, 0, 2))[:, :, :, None] * gain_block[:, None, None, :]
        return jnp.zeros((ST_DEV, 2, NF, M), jnp.float32).at[local].add(outer)

    def rows_of(table, block):
        return lax.dynamic_slice_in_dim(table, (block * ST_DEV).astype(jnp.int32), ST_DEV, 0)

    def down_step(state, inputs):
        term, rate = inputs
        state = cmul(rate[None, None, :] * rot_down, state) + term
        return (state, state)

    def up_step(state, inputs):
        term, rate = inputs
        state = cmul(rate[None, None, :] * rot_up, state) + term
        return (state, state)

    def first_pass(entering, block):
        forcing = block_forcing(block)
        leaving, unused = lax.scan(down_step, entering, (forcing, rows_of(damping, block)))
        return (leaving, entering)
    final_down, entering_all = lax.scan(first_pass, zeros, jnp.arange(n_blocks, dtype=jnp.int32))

    def second_pass(entering_up, inputs):
        block, entering_down = inputs
        forcing = block_forcing(block)
        leaving_up, upstream = lax.scan(up_step, entering_up, (forcing, rows_of(damping_up, block)), reverse=True)
        unused, downstream = lax.scan(down_step, entering_down, (forcing, rows_of(damping, block)))
        state = (downstream + upstream).astype(jnp.bfloat16)
        estimator_answer = jnp.einsum('kcfm,cft->kmt', state.astype(jnp.float32), inverse.astype(jnp.float32)).astype(jnp.bfloat16)
        return (leaving_up, estimator_answer)
    final_up, blocks_out = lax.scan(second_pass, zeros, (jnp.arange(n_blocks, dtype=jnp.int32), entering_all), reverse=True)
    return blocks_out.reshape(STATIONS, M, TOUT)
```

```python
import functools
import math

import jax
import jax.numpy as jnp
from jax import lax
from jax.experimental import pallas as pl
from jax.experimental.pallas import tpu as pltpu
from jax.sharding import PartitionSpec as P

NT = 16384
NF = 1024
TOUT = 1024
CHUNKS = 3
TILE = 128
SUB = 16
F32 = jnp.float32
BF16 = jnp.bfloat16


def shifted(block, axis, distance):
    devices = range(lax.axis_size(axis))
    route = [(i - distance, i) for i in devices if i - distance in devices]
    return lax.ppermute(block, axis, route)


def cmul(left, right):
    return (left[0] * right[0] - left[1] * right[1], left[0] * right[1] + left[1] * right[0])


def cpow(base, n):
    out = None
    while n:
        if n & 1:
            out = base if out is None else cmul(out, base)
        n >>= 1
        if n:
            base = cmul(base, base)
    return out


def angles(left, right):
    return (left * right % NT).astype(F32) * (2 * math.pi / NT)


def spectrum_kernel(x_ref, lc_ref, ls_ref, hc_ref, hs_ref, out_ref):
    hc, hs = hc_ref[...], hs_ref[...]
    re, im = [], []
    for s in range(x_ref.shape[0]):
        a = jnp.dot(x_ref[s], lc_ref[...], preferred_element_type=F32)
        b = jnp.dot(x_ref[s], ls_ref[...], preferred_element_type=F32)
        re.append(jnp.sum(hc * a - hs * b, axis=0, keepdims=True))
        im.append(-jnp.sum(hs * a + hc * b, axis=0, keepdims=True))
    scale = 1.0 / math.sqrt(NT)
    out_ref[0] = (jnp.concatenate(re, axis=0) * scale).astype(BF16)
    out_ref[1] = (jnp.concatenate(im, axis=0) * scale).astype(BF16)


def spectrum(signals, freq_bins):
    sens = signals.shape[0]
    fine = 128
    coarse = NT // fine
    times = lax.iota(jnp.int32, NT)
    hann = 0.5 - 0.5 * jnp.cos(times.astype(F32) * (2 * math.pi / NT))
    windowed = (signals.astype(F32) * hann[None, :]).astype(BF16).reshape(sens, coarse, fine)
    low = angles(lax.iota(jnp.int32, fine)[:, None], freq_bins[None, :])
    high = angles(lax.iota(jnp.int32, coarse)[:, None] * fine, freq_bins[None, :])
    ft = 256
    table = pl.BlockSpec((fine, ft), lambda i: (0, i))
    big = pl.BlockSpec((coarse, ft), lambda i: (0, i))
    return pl.pallas_call(
        spectrum_kernel,
        grid=(NF // ft,),
        in_specs=[pl.BlockSpec((sens, coarse, fine), lambda i: (0, 0, 0)), table, table, big, big],
        out_specs=pl.BlockSpec((2, sens, ft), lambda i: (0, 0, i)),
        out_shape=jax.ShapeDtypeStruct((2, sens, NF), BF16),
        cost_estimate=pl.CostEstimate(
            flops=4 * sens * NT * NF, bytes_accessed=4 << 20, transcendentals=0
        ),
        name="spectrum",
    )(windowed, jnp.cos(low).astype(BF16), jnp.sin(low).astype(BF16), jnp.cos(high), jnp.sin(high))


def step_down(state, rate, c, s, fr, fi):
    re, im = state
    return (rate * (re * c + im * s) + fr, rate * (im * c - re * s) + fi)


def step_up(state, rate, c, s, fr, fi):
    re, im = state
    return (rate * (re * c - im * s) + fr, rate * (im * c + re * s) + fi)


def ends_kernel(own, mg_ref, spec_ref, c_ref, s_ref, dd_ref, du_ref, down_ref, up_ref, f_ref):
    count, tile, sens = mg_ref.shape
    fd = c_ref.shape[1]

    def sub(i, unused):
        rows = pl.ds(pl.multiple_of(i * SUB, SUB), SUB)
        left = mg_ref[:, rows, :].reshape(count * SUB, sens)
        f_ref[...] = jnp.dot(left, spec_ref[...], preferred_element_type=F32).reshape(
            count, SUB, 2 * fd
        )
        c, s = c_ref[rows, :], s_ref[rows, :]
        rd, ru = dd_ref[rows, :], du_ref[rows, :]
        down = up = (jnp.zeros((SUB, fd), F32), jnp.zeros((SUB, fd), F32))
        for k in range(count):
            down = step_down(down, rd[:, k : k + 1], c, s, f_ref[k, :, :fd], f_ref[k, :, fd:])
            b = count - 1 - k
            up = step_up(up, ru[:, b : b + 1], c, s, f_ref[b, :, :fd], f_ref[b, :, fd:])
            if (k + 1) % own == 0:
                q = (k + 1) // own - 1
                down_ref[q, 0, rows, :], down_ref[q, 1, rows, :] = down
                up_ref[q, 0, rows, :], up_ref[q, 1, rows, :] = up
        return unused

    lax.fori_loop(0, tile // SUB, sub, 0)


def block_ends(own, mg, spec, c, s, dd, du):
    count, width, sens = mg.shape
    fd = c.shape[1]
    parts = count // own
    tiles = width // TILE
    row = lambda i: (i, 0)
    out = jax.ShapeDtypeStruct((parts, 2, tiles * TILE, fd), F32)
    out_spec = pl.BlockSpec((parts, 2, TILE, fd), lambda i: (0, 0, i, 0))
    return pl.pallas_call(
        functools.partial(ends_kernel, own),
        grid=(tiles,),
        in_specs=[
            pl.BlockSpec((count, TILE, sens), lambda i: (0, i, 0)),
            pl.BlockSpec((sens, 2 * fd), lambda i: (0, 0)),
            pl.BlockSpec((TILE, fd), row),
            pl.BlockSpec((TILE, fd), row),
            pl.BlockSpec((TILE, count), row),
            pl.BlockSpec((TILE, count), row),
        ],
        out_specs=[out_spec, out_spec],
        out_shape=[out, out],
        scratch_shapes=[pltpu.VMEM((count, SUB, 2 * fd), F32)],
        cost_estimate=pl.CostEstimate(
            flops=8 * 256 * count * tiles * TILE * fd, bytes_accessed=8 << 20, transcendentals=0
        ),
        name="block_ends",
    )(mg, spec, c, s, dd, du)


def march_kernel(mg_ref, spec_ref, c_ref, s_ref, dd_ref, du_ref, in_ref, inv_ref, *rest):
    out_ref, f_ref, d_ref, state_ref = rest[-4:]
    own, tile, sens = mg_ref.shape
    parts, _, _, fd = in_ref.shape

    def sub(i, unused):
        rows = pl.ds(pl.multiple_of(i * SUB, SUB), SUB)
        left = mg_ref[:, rows, :].reshape(own * SUB, sens)
        f_ref[...] = jnp.dot(left, spec_ref[...], preferred_element_type=F32).reshape(
            own, SUB, 2 * NF
        )
        rd, ru = dd_ref[rows, :], du_ref[rows, :]
        for j in range(parts):
            lo, hi = slice(j * fd, (j + 1) * fd), slice(NF + j * fd, NF + (j + 1) * fd)
            c, s = c_ref[rows, lo], s_ref[rows, lo]
            down = (in_ref[j, 0, rows, :].astype(F32), in_ref[j, 1, rows, :].astype(F32))
            for k in range(own):
                down = step_down(down, rd[:, k : k + 1], c, s, f_ref[k, :, lo], f_ref[k, :, hi])
                d_ref[k, 0], d_ref[k, 1] = down
            up = (in_ref[j, 2, rows, :].astype(F32), in_ref[j, 3, rows, :].astype(F32))
            for k in reversed(range(own)):
                up = step_up(up, ru[:, k : k + 1], c, s, f_ref[k, :, lo], f_ref[k, :, hi])
                state_ref[k, rows, lo] = (d_ref[k, 0] + up[0]).astype(BF16)
                state_ref[k, rows, hi] = (d_ref[k, 1] + up[1]).astype(BF16)
        return unused

    lax.fori_loop(0, tile // SUB, sub, 0)
    step = 256

    def columns(n, unused):
        cols = pl.ds(pl.multiple_of(n * step, step), step)
        got = jnp.dot(
            state_ref[...].reshape(own * tile, 2 * NF),
            inv_ref[:, cols],
            preferred_element_type=F32,
        )
        out_ref[:, :, cols] = got.reshape(own, tile, step).astype(BF16)
        return unused

    lax.fori_loop(0, TOUT // step, columns, 0)


def estimate_chunk(chunk, mg, spec, c, s, dd, du, entering, inverse, filled):
    own, width, sens = mg.shape
    parts, _, wide, fd = entering.shape
    tiles = wide // TILE
    row = lambda i: (chunk * tiles + i, 0)
    specs = [
        pl.BlockSpec((own, TILE, sens), lambda i: (0, chunk * tiles + i, 0)),
        pl.BlockSpec((sens, 2 * NF), lambda i: (0, 0)),
        pl.BlockSpec((TILE, NF), row),
        pl.BlockSpec((TILE, NF), row),
        pl.BlockSpec((TILE, own), row),
        pl.BlockSpec((TILE, own), row),
        pl.BlockSpec((parts, 4, TILE, fd), lambda i: (0, 0, i, 0)),
        pl.BlockSpec((2 * NF, TOUT), lambda i: (0, 0)),
    ]
    args = [mg, spec, c, s, dd, du, entering, inverse]
    aliases = {}
    if filled is not None:
        aliases = {len(args): 0}
        specs.append(pl.BlockSpec(memory_space=pl.ANY))
        args.append(filled)
    return pl.pallas_call(
        march_kernel,
        grid=(tiles,),
        in_specs=specs,
        out_specs=pl.BlockSpec((own, TILE, TOUT), lambda i: (0, chunk * tiles + i, 0)),
        out_shape=jax.ShapeDtypeStruct((own, width, TOUT), BF16),
        scratch_shapes=[
            pltpu.VMEM((own, SUB, 2 * NF), F32),
            pltpu.VMEM((own, 2, SUB, fd), F32),
            pltpu.VMEM((own, TILE, 2 * NF), BF16),
        ],
        input_output_aliases=aliases,
        cost_estimate=pl.CostEstimate(
            flops=12 * own * wide * NF * TOUT, bytes_accessed=16 << 20, transcendentals=0
        ),
        name="march",
    )(*args)


def masked_gain(local, first, count, gain_t):
    stations = first + lax.iota(jnp.int32, count)
    hit = local[None, None, :] == stations[:, None, None]
    return jnp.where(hit, gain_t[None], jnp.zeros((), BF16))


def rotation(freq_bins, phase_speed):
    turn = 2 * math.pi * (freq_bins.astype(F32) / NT)
    theta = phase_speed[:, None] * turn[None, :]
    return jnp.cos(theta), jnp.sin(theta)


def inverse_table(freq_bins):
    fine = 128
    low = angles(freq_bins[:, None], lax.iota(jnp.int32, fine)[None, :])
    steps = NT - TOUT + fine * lax.iota(jnp.int32, TOUT // fine)
    high = angles(freq_bins[:, None], steps[None, :])
    lc, ls, hc, hs = lax.optimization_barrier(
        (jnp.cos(low), jnp.sin(low), jnp.cos(high), jnp.sin(high))
    )
    scale = 1.0 / math.sqrt(NF)
    hc, hs = hc * scale, hs * scale
    cosines, sines = [], []
    for h in range(TOUT // fine):
        a, b = hc[:, h : h + 1], hs[:, h : h + 1]
        cosines.append((a * lc - b * ls).astype(BF16))
        sines.append((-(b * lc + a * ls)).astype(BF16))
    return jnp.concatenate(
        [jnp.concatenate(cosines, axis=1), jnp.concatenate(sines, axis=1)], axis=0
    )


def on_device(signals, freq_bins, sensor_station, gain, damping, damping_up, phase_speed):
    parts = lax.axis_size("fq")
    mine = lax.axis_index("fq")
    st_dev, width = damping.shape
    own = st_dev // parts
    fd = NF // parts
    sens = gain.shape[0]

    spec = spectrum(signals, freq_bins)
    spec = lax.all_to_all(
        jnp.broadcast_to(spec[None], (parts,) + spec.shape), "fq", 0, 0, tiled=True
    )
    spec = spec.transpose(0, 2, 1, 3).reshape(sens, 2, NF)
    spec_own = lax.dynamic_slice_in_dim(spec, mine * fd, fd, 2).reshape(sens, 2 * fd)
    spec = spec.reshape(sens, 2 * NF)

    own_bins = lax.dynamic_slice_in_dim(freq_bins, mine * fd, fd)
    c, s = rotation(own_bins, phase_speed)
    local = sensor_station - lax.axis_index("st") * st_dev
    gain_t = gain.T
    mg = masked_gain(local, 0, st_dev, gain_t)
    dd, du = damping.T, damping_up.T
    chunk_width = width // CHUNKS

    c_all, s_all = rotation(freq_bins, phase_speed)
    mg_own = masked_gain(local, mine * own, own, gain_t)
    dd_own = lax.dynamic_slice_in_dim(dd, mine * own, own, 1)
    du_own = lax.dynamic_slice_in_dim(du, mine * own, own, 1)
    inverse = inverse_table(freq_bins)

    down_loc, up_loc = block_ends(own, mg, spec_own, c, s, dd, du)
    unit = cpow((c, s), own)
    turns = [unit]
    for j in range(1, parts):
        turns.append(cmul(turns[-1], unit))
    turns = lax.optimization_barrier(turns)

    def down_factor(j):
        rate = jnp.prod(damping[: j * own], axis=0)[:, None]
        return (rate * turns[j - 1][0], -rate * turns[j - 1][1])

    def up_factor(j):
        rate = jnp.prod(damping_up[st_dev - j * own :], axis=0)[:, None]
        return (rate * turns[j - 1][0], rate * turns[j - 1][1])

    full_down, full_up = lax.optimization_barrier((down_factor(parts), up_factor(parts)))
    below = above = jnp.zeros((2, width, fd), F32)
    for hop in range(lax.axis_size("st") - 1):
        out_down = jnp.stack(cmul(full_down, below)) + down_loc[parts - 1]
        out_up = jnp.stack(cmul(full_up, above)) + up_loc[parts - 1]
        below = shifted(out_down.astype(BF16), "st", 1).astype(F32)
        above = shifted(out_up.astype(BF16), "st", -1).astype(F32)
    entering = []
    for i in range(CHUNKS):
        rows = slice(i * chunk_width, (i + 1) * chunk_width)
        pieces = []
        for q in range(parts):
            down_in, up_in = below[:, rows], above[:, rows]
            if q > 0:
                down_in = (jnp.stack(cmul(down_factor(q), below)) + down_loc[q - 1])[:, rows]
            if q < parts - 1:
                lifted = jnp.stack(cmul(up_factor(parts - 1 - q), above))
                up_in = (lifted + up_loc[parts - 2 - q])[:, rows]
            pieces.append(jnp.concatenate([down_in, up_in], axis=0).astype(BF16))
        entering.append(lax.all_to_all(jnp.stack(pieces), "fq", 0, 0, tiled=True))

    result = None
    for i in range(CHUNKS):
        result = estimate_chunk(
            i, mg_own, spec, c_all, s_all, dd_own, du_own, entering[i], inverse, result
        )
    return result


def solution(mesh):
    placed = (P(("st", "fq"), None), P(), P("st"), P("st", None), P("st", None), P("st", None), P())
    return jax.shard_map(
        on_device,
        mesh=mesh,
        in_specs=placed,
        out_specs=P(("st", "fq"), None, None),
        check_vma=False,
    )
```

```python
import functools
import math

import jax
import jax.numpy as jnp
from jax import lax
from jax.experimental import pallas as pl
from jax.experimental.pallas import tpu as pltpu
from jax.sharding import PartitionSpec as P

NT = 16384
NF = 1024
TOUT = 1024
CHUNKS = 3
TILE = 128
SUB = 16
F32 = jnp.float32
BF16 = jnp.bfloat16


def cmul(left, right):
    return (left[0] * right[0] - left[1] * right[1], left[0] * right[1] + left[1] * right[0])


def cpow(base, n):
    out = None
    while n:
        if n & 1:
            out = base if out is None else cmul(out, base)
        n >>= 1
        if n:
            base = cmul(base, base)
    return out


def angles(left, right):
    return (left * right % NT).astype(F32) * (2 * math.pi / NT)


def spectrum_kernel(x_ref, lc_ref, ls_ref, hc_ref, hs_ref, out_ref):
    hc, hs = hc_ref[...], hs_ref[...]
    re, im = [], []
    for s in range(x_ref.shape[0]):
        a = jnp.dot(x_ref[s], lc_ref[...], preferred_element_type=F32)
        b = jnp.dot(x_ref[s], ls_ref[...], preferred_element_type=F32)
        re.append(jnp.sum(hc * a - hs * b, axis=0, keepdims=True))
        im.append(-jnp.sum(hs * a + hc * b, axis=0, keepdims=True))
    scale = 1.0 / math.sqrt(NT)
    out_ref[0] = (jnp.concatenate(re, axis=0) * scale).astype(BF16)
    out_ref[1] = (jnp.concatenate(im, axis=0) * scale).astype(BF16)


def spectrum(signals, freq_bins):
    sens = signals.shape[0]
    fine = 128
    coarse = NT // fine
    times = lax.iota(jnp.int32, NT)
    hann = 0.5 - 0.5 * jnp.cos(times.astype(F32) * (2 * math.pi / NT))
    windowed = (signals.astype(F32) * hann[None, :]).astype(BF16).reshape(sens, coarse, fine)
    low = angles(lax.iota(jnp.int32, fine)[:, None], freq_bins[None, :])
    high = angles(lax.iota(jnp.int32, coarse)[:, None] * fine, freq_bins[None, :])
    ft = 256
    table = pl.BlockSpec((fine, ft), lambda i: (0, i))
    big = pl.BlockSpec((coarse, ft), lambda i: (0, i))
    return pl.pallas_call(
        spectrum_kernel,
        grid=(NF // ft,),
        in_specs=[pl.BlockSpec((sens, coarse, fine), lambda i: (0, 0, 0)), table, table, big, big],
        out_specs=pl.BlockSpec((2, sens, ft), lambda i: (0, 0, i)),
        out_shape=jax.ShapeDtypeStruct((2, sens, NF), BF16),
        cost_estimate=pl.CostEstimate(
            flops=4 * sens * NT * NF, bytes_accessed=4 << 20, transcendentals=0
        ),
        name="spectrum",
    )(windowed, jnp.cos(low).astype(BF16), jnp.sin(low).astype(BF16), jnp.cos(high), jnp.sin(high))


def step_down(state, rate, c, s, fr, fi):
    re, im = state
    return (rate * (re * c + im * s) + fr, rate * (im * c - re * s) + fi)


def step_up(state, rate, c, s, fr, fi):
    re, im = state
    return (rate * (re * c - im * s) + fr, rate * (im * c + re * s) + fi)


def ends_kernel(own, mg_ref, spec_ref, c_ref, s_ref, dd_ref, du_ref, down_ref, up_ref, f_ref):
    count, tile, sens = mg_ref.shape
    fd = c_ref.shape[1]

    def sub(i, unused):
        rows = pl.ds(pl.multiple_of(i * SUB, SUB), SUB)
        left = mg_ref[:, rows, :].reshape(count * SUB, sens)
        f_ref[...] = jnp.dot(left, spec_ref[...], preferred_element_type=F32).reshape(
            count, SUB, 2 * fd
        )
        c, s = c_ref[rows, :], s_ref[rows, :]
        rd, ru = dd_ref[rows, :], du_ref[rows, :]
        down = up = (jnp.zeros((SUB, fd), F32), jnp.zeros((SUB, fd), F32))
        for k in range(count):
            down = step_down(down, rd[:, k : k + 1], c, s, f_ref[k, :, :fd], f_ref[k, :, fd:])
            b = count - 1 - k
            up = step_up(up, ru[:, b : b + 1], c, s, f_ref[b, :, :fd], f_ref[b, :, fd:])
            if (k + 1) % own == 0:
                q = (k + 1) // own - 1
                down_ref[q, 0, rows, :], down_ref[q, 1, rows, :] = down
                up_ref[q, 0, rows, :], up_ref[q, 1, rows, :] = up
        return unused

    lax.fori_loop(0, tile // SUB, sub, 0)


def block_ends(own, mg, spec, c, s, dd, du):
    count, width, sens = mg.shape
    fd = c.shape[1]
    parts = count // own
    tiles = width // TILE
    row = lambda i: (i, 0)
    out = jax.ShapeDtypeStruct((parts, 2, tiles * TILE, fd), F32)
    out_spec = pl.BlockSpec((parts, 2, TILE, fd), lambda i: (0, 0, i, 0))
    return pl.pallas_call(
        functools.partial(ends_kernel, own),
        grid=(tiles,),
        in_specs=[
            pl.BlockSpec((count, TILE, sens), lambda i: (0, i, 0)),
            pl.BlockSpec((sens, 2 * fd), lambda i: (0, 0)),
            pl.BlockSpec((TILE, fd), row),
            pl.BlockSpec((TILE, fd), row),
            pl.BlockSpec((TILE, count), row),
            pl.BlockSpec((TILE, count), row),
        ],
        out_specs=[out_spec, out_spec],
        out_shape=[out, out],
        scratch_shapes=[pltpu.VMEM((count, SUB, 2 * fd), F32)],
        cost_estimate=pl.CostEstimate(
            flops=8 * 256 * count * tiles * TILE * fd, bytes_accessed=8 << 20, transcendentals=0
        ),
        name="block_ends",
    )(mg, spec, c, s, dd, du)


def relay_kernel(
    fac_down, last_down, fac_up, last_up, below, above, out_down, out_up, sd, rd, su, ru
):
    n, me = lax.axis_size("st"), lax.axis_index("st")
    right, left = lax.rem(me + 1, n), lax.rem(me + n - 1, n)
    count = below.shape[1] // TILE
    barrier = pltpu.get_barrier_semaphore()
    for neighbour in (left, right):
        pl.semaphore_signal(
            barrier, inc=1, device_id={"st": neighbour}, device_id_type=pl.DeviceIdType.MESH
        )
    pl.semaphore_wait(barrier, 2)

    def rows_of(p):
        return pl.ds(pl.multiple_of(p * TILE, TILE), TILE)

    def copy(p, source, target, send, recv, device):
        return pltpu.make_async_remote_copy(
            src_ref=source.at[:, rows_of(p), :],
            dst_ref=target.at[:, rows_of(p), :],
            send_sem=send.at[p],
            recv_sem=recv.at[p],
            device_id={"st": device},
            device_id_type=pl.DeviceIdType.MESH,
        )

    def down_copy(p):
        return copy(p, out_down, below, sd, rd, right)

    def up_copy(p):
        return copy(p, out_up, above, su, ru, left)

    def visit(p, first, final, moved, entering, factor, last, leaving):
        @pl.when((p >= 0) & (p < count))
        def _():
            rows = rows_of(p)

            @pl.when(first)
            def _():
                entering[:, rows, :] = jnp.zeros((2, TILE, entering.shape[2]), BF16)

            @pl.when(jnp.logical_not(first))
            def _():
                moved(p).wait_recv()

            @pl.when(jnp.logical_not(final))
            def _():
                state = (entering[0, rows, :].astype(F32), entering[1, rows, :].astype(F32))
                re, im = cmul((factor[0, rows, :], factor[1, rows, :]), state)
                leaving[0, rows, :] = (re + last[0, rows, :]).astype(BF16)
                leaving[1, rows, :] = (im + last[1, rows, :]).astype(BF16)
                moved(p).start()

    def turn(t, unused):
        bottom, top = me == 0, me == n - 1
        visit(t - me, bottom, top, down_copy, below, fac_down, last_down, out_down)
        visit(t - (n - 1 - me), top, bottom, up_copy, above, fac_up, last_up, out_up)
        return unused

    lax.fori_loop(0, n - 1 + count, turn, 0)

    def finish(p, unused):
        @pl.when(me < n - 1)
        def _():
            down_copy(p).wait_send()

        @pl.when(me > 0)
        def _():
            up_copy(p).wait_send()

        return unused

    lax.fori_loop(0, count, finish, 0)


def relay(fac_down, last_down, fac_up, last_up):
    _, width, fd = last_down.shape
    vmem = pl.BlockSpec(memory_space=pltpu.VMEM)
    out = jax.ShapeDtypeStruct((2, width, fd), BF16)
    sems = pltpu.SemaphoreType.DMA((width // TILE,))
    return pl.pallas_call(
        relay_kernel,
        in_specs=[vmem] * 4,
        out_specs=[vmem] * 2,
        out_shape=[out, out],
        scratch_shapes=[pltpu.VMEM((2, width, fd), BF16)] * 2 + [sems] * 4,
        compiler_params=pltpu.CompilerParams(collective_id=0, has_side_effects=True),
        name="relay",
    )(fac_down, last_down, fac_up, last_up)


def march_kernel(mg_ref, spec_ref, c_ref, s_ref, dd_ref, du_ref, in_ref, inv_ref, *rest):
    out_ref, f_ref, d_ref, state_ref = rest[-4:]
    own, tile, sens = mg_ref.shape
    parts, _, _, fd = in_ref.shape

    def sub(i, unused):
        rows = pl.ds(pl.multiple_of(i * SUB, SUB), SUB)
        left = mg_ref[:, rows, :].reshape(own * SUB, sens)
        f_ref[...] = jnp.dot(left, spec_ref[...], preferred_element_type=F32).reshape(
            own, SUB, 2 * NF
        )
        rd, ru = dd_ref[rows, :], du_ref[rows, :]
        for j in range(parts):
            lo, hi = slice(j * fd, (j + 1) * fd), slice(NF + j * fd, NF + (j + 1) * fd)
            c, s = c_ref[rows, lo], s_ref[rows, lo]
            down = (in_ref[j, 0, rows, :].astype(F32), in_ref[j, 1, rows, :].astype(F32))
            for k in range(own):
                down = step_down(down, rd[:, k : k + 1], c, s, f_ref[k, :, lo], f_ref[k, :, hi])
                d_ref[k, 0], d_ref[k, 1] = down
            up = (in_ref[j, 2, rows, :].astype(F32), in_ref[j, 3, rows, :].astype(F32))
            for k in reversed(range(own)):
                up = step_up(up, ru[:, k : k + 1], c, s, f_ref[k, :, lo], f_ref[k, :, hi])
                state_ref[k, rows, lo] = (d_ref[k, 0] + up[0]).astype(BF16)
                state_ref[k, rows, hi] = (d_ref[k, 1] + up[1]).astype(BF16)
        return unused

    lax.fori_loop(0, tile // SUB, sub, 0)
    step = 256

    def columns(n, unused):
        cols = pl.ds(pl.multiple_of(n * step, step), step)
        got = jnp.dot(
            state_ref[...].reshape(own * tile, 2 * NF),
            inv_ref[:, cols],
            preferred_element_type=F32,
        )
        out_ref[:, :, cols] = got.reshape(own, tile, step).astype(BF16)
        return unused

    lax.fori_loop(0, TOUT // step, columns, 0)


def estimate_chunk(chunk, mg, spec, c, s, dd, du, entering, inverse, filled):
    own, width, sens = mg.shape
    parts, _, wide, fd = entering.shape
    tiles = wide // TILE
    row = lambda i: (chunk * tiles + i, 0)
    specs = [
        pl.BlockSpec((own, TILE, sens), lambda i: (0, chunk * tiles + i, 0)),
        pl.BlockSpec((sens, 2 * NF), lambda i: (0, 0)),
        pl.BlockSpec((TILE, NF), row),
        pl.BlockSpec((TILE, NF), row),
        pl.BlockSpec((TILE, own), row),
        pl.BlockSpec((TILE, own), row),
        pl.BlockSpec((parts, 4, TILE, fd), lambda i: (0, 0, i, 0)),
        pl.BlockSpec((2 * NF, TOUT), lambda i: (0, 0)),
    ]
    args = [mg, spec, c, s, dd, du, entering, inverse]
    aliases = {}
    if filled is not None:
        aliases = {len(args): 0}
        specs.append(pl.BlockSpec(memory_space=pl.ANY))
        args.append(filled)
    return pl.pallas_call(
        march_kernel,
        grid=(tiles,),
        in_specs=specs,
        out_specs=pl.BlockSpec((own, TILE, TOUT), lambda i: (0, chunk * tiles + i, 0)),
        out_shape=jax.ShapeDtypeStruct((own, width, TOUT), BF16),
        scratch_shapes=[
            pltpu.VMEM((own, SUB, 2 * NF), F32),
            pltpu.VMEM((own, 2, SUB, fd), F32),
            pltpu.VMEM((own, TILE, 2 * NF), BF16),
        ],
        input_output_aliases=aliases,
        cost_estimate=pl.CostEstimate(
            flops=12 * own * wide * NF * TOUT, bytes_accessed=16 << 20, transcendentals=0
        ),
        name="march",
    )(*args)


def masked_gain(local, first, count, gain_t):
    stations = first + lax.iota(jnp.int32, count)
    hit = local[None, None, :] == stations[:, None, None]
    return jnp.where(hit, gain_t[None], jnp.zeros((), BF16))


def rotation(freq_bins, phase_speed):
    turn = 2 * math.pi * (freq_bins.astype(F32) / NT)
    theta = phase_speed[:, None] * turn[None, :]
    return jnp.cos(theta), jnp.sin(theta)


def inverse_table(freq_bins):
    fine = 128
    low = angles(freq_bins[:, None], lax.iota(jnp.int32, fine)[None, :])
    steps = NT - TOUT + fine * lax.iota(jnp.int32, TOUT // fine)
    high = angles(freq_bins[:, None], steps[None, :])
    lc, ls, hc, hs = lax.optimization_barrier(
        (jnp.cos(low), jnp.sin(low), jnp.cos(high), jnp.sin(high))
    )
    scale = 1.0 / math.sqrt(NF)
    hc, hs = hc * scale, hs * scale
    cosines, sines = [], []
    for h in range(TOUT // fine):
        a, b = hc[:, h : h + 1], hs[:, h : h + 1]
        cosines.append((a * lc - b * ls).astype(BF16))
        sines.append((-(b * lc + a * ls)).astype(BF16))
    return jnp.concatenate(
        [jnp.concatenate(cosines, axis=1), jnp.concatenate(sines, axis=1)], axis=0
    )


def on_device(signals, freq_bins, sensor_station, gain, damping, damping_up, phase_speed):
    parts = lax.axis_size("fq")
    mine = lax.axis_index("fq")
    st_dev, width = damping.shape
    own = st_dev // parts
    fd = NF // parts
    sens = gain.shape[0]

    spec = spectrum(signals, freq_bins)
    spec = lax.all_to_all(
        jnp.broadcast_to(spec[None], (parts,) + spec.shape), "fq", 0, 0, tiled=True
    )
    spec = spec.transpose(0, 2, 1, 3).reshape(sens, 2, NF)
    spec_own = lax.dynamic_slice_in_dim(spec, mine * fd, fd, 2).reshape(sens, 2 * fd)
    spec = spec.reshape(sens, 2 * NF)

    own_bins = lax.dynamic_slice_in_dim(freq_bins, mine * fd, fd)
    c, s = rotation(own_bins, phase_speed)
    local = sensor_station - lax.axis_index("st") * st_dev
    gain_t = gain.T
    mg = masked_gain(local, 0, st_dev, gain_t)
    dd, du = damping.T, damping_up.T
    chunk_width = width // CHUNKS

    c_all, s_all = rotation(freq_bins, phase_speed)
    mg_own = masked_gain(local, mine * own, own, gain_t)
    dd_own = lax.dynamic_slice_in_dim(dd, mine * own, own, 1)
    du_own = lax.dynamic_slice_in_dim(du, mine * own, own, 1)
    inverse = inverse_table(freq_bins)

    down_loc, up_loc = block_ends(own, mg, spec_own, c, s, dd, du)
    unit = cpow((c, s), own)
    turns = [unit]
    for j in range(1, parts):
        turns.append(cmul(turns[-1], unit))
    turns = lax.optimization_barrier(turns)

    def down_factor(j):
        rate = jnp.prod(damping[: j * own], axis=0)[:, None]
        return (rate * turns[j - 1][0], -rate * turns[j - 1][1])

    def up_factor(j):
        rate = jnp.prod(damping_up[st_dev - j * own :], axis=0)[:, None]
        return (rate * turns[j - 1][0], rate * turns[j - 1][1])

    full_down, full_up = jnp.stack(down_factor(parts)), jnp.stack(up_factor(parts))
    below, above = relay(full_down, down_loc[parts - 1], full_up, up_loc[parts - 1])
    below, above = below.astype(F32), above.astype(F32)
    def march(i, filled):
        return estimate_chunk(
            i, mg_own, spec, c_all, s_all, dd_own, du_own, entering[i], inverse, filled
        )

    entering = []
    result = None
    for i in range(CHUNKS):
        rows = slice(i * chunk_width, (i + 1) * chunk_width)
        pieces = []
        for q in range(parts):
            down_in, up_in = below[:, rows], above[:, rows]
            if q > 0:
                down_in = (jnp.stack(cmul(down_factor(q), below)) + down_loc[q - 1])[:, rows]
            if q < parts - 1:
                lifted = jnp.stack(cmul(up_factor(parts - 1 - q), above))
                up_in = (lifted + up_loc[parts - 2 - q])[:, rows]
            pieces.append(jnp.concatenate([down_in, up_in], axis=0).astype(BF16))
        leaving = jnp.stack(pieces)
        if i == 1:
            leaving, c_all, s_all, inverse = lax.optimization_barrier(
                (leaving, c_all, s_all, inverse)
            )
        if i >= 2:
            result = march(i - 2, result)
            leaving, result = lax.optimization_barrier((leaving, result))
        entering.append(lax.all_to_all(leaving, "fq", 0, 0, tiled=True))

    for i in range(max(CHUNKS - 2, 0), CHUNKS):
        result = march(i, result)
    return result


def solution(mesh):
    placed = (P(("st", "fq"), None), P(), P("st"), P("st", None), P("st", None), P("st", None), P())
    return jax.shard_map(
        on_device,
        mesh=mesh,
        in_specs=placed,
        out_specs=P(("st", "fq"), None, None),
        check_vma=False,
    )
```
